256 devices in a mesh: gz: 4 (over y_hi, core), gy: 8 (over z), gx: 8 (over y_lo, x).
Axes of the slice: x: 4, y: 4 (y_hi: 2, y_lo: 2; y = y_hi * 2 + y_lo), z: 8, core: 2. Of those that a mesh axis runs over, the one named last changes fastest.
Arguments:
- raw_views: float32 [4, 32, 128, 1024], P(None, 'gz', 'gy', 'gx'), may hold values from 0.25 to 4
- interp_weight: float32 [4, 1024], replicated, may hold values from 0 to 1
- sample_index: int32 [4, 1024], replicated, may hold values from 0 to 1022, as said below
- psf: float32 [4, 3, 4, 9], replicated, may hold values from 0.05 to 1
- estimate: float32 [32, 128, 1024], P('gz', 'gy', 'gx'), may hold values from 0.5 to 2
Outputs:
- restored: float32 [32, 128, 1024], P('gz', 'gy', 'gx')
The draws below stay inside these ranges and needn't reach their ends.
Inputs may be any that keep to these rules, and one draw needn't show every extreme that they name: sample_index[v, x] and sample_index[v, x] + 1 lie in the brick of 128 columns that holds column x or in one of the two bricks beside it; every view reads from a brick beside for some columns.
All inputs are finite; a program needn't handle non-finite values.
Results may differ from the reference program's by a relative error of at most 0.00005.
Values sent between devices are 32-bit elements; how exact they have to be, the bound alone decides.
A program may use at most 64 MiB of HBM per device.

```python
import math
import jax
import jax.numpy as jnp
from jax import lax

V = 4
RANK = 4
TAPS = 9
ITERS = 1
CX = 128
NZ = 32
NY = 128
NX = 1024


def draw_sample_index(key, part):
    key_scale, key_shift = jax.random.split(key, 2)
    scale_num = jax.random.randint(key_scale, (V,), -(CX // 2), CX // 2 + 1, dtype=jnp.int32)
    shift_size = jax.random.randint(key_shift, (V,), CX // 8 + 2, CX // 4 + 2, dtype=jnp.int32)
    signs = jnp.where(jnp.arange(V, dtype=jnp.int32) % 2 == 0, 1, -1).astype(jnp.int32)
    shifts = shift_size * signs
    columns_all = jnp.arange(NX, dtype=jnp.int32)
    centre = NX // 2
    denom = 2 * NX
    offsets = columns_all[None, :] - centre
    position = offsets * (denom + scale_num[:, None]) // denom + centre + shifts[:, None]
    return jnp.clip(position, 0, NX - 2).astype(jnp.int32)


def shard_levels(stream_key, extent, cuts, smallest, high):
    factor_of, own = 1.0, jax.random.fold_in(stream_key, 6)
    for dim, shards_of in cuts:
        heights = jnp.exp(jax.random.uniform(jax.random.fold_in(own, dim), (shards_of,), jnp.float32, smallest / len(cuts), high / len(cuts)))
        factor_of = factor_of * jnp.repeat(heights, extent[dim] // shards_of).reshape([-1 if axis == dim else 1 for axis in range(len(extent))])
    return factor_of


def setup_inputs(seed: int = 0) -> dict:
    keys = jax.random.split(jax.random.key(seed), 6)
    return {
        "raw_views": jnp.clip(jnp.exp(math.log(4.0) - 2.7725887 * jax.random.uniform(keys[0], (V, NZ, NY, NX), jnp.float32) ** shard_levels(keys[0], (V, NZ, NY, NX), ((1, 4), (2, 8), (3, 8)), -0.2, 0.2)), 0.25, 4.0),
        "interp_weight": jnp.clip(jax.random.uniform(keys[1], (V, NX), jnp.float32, 0.0, 1.0), 0.0, 1.0),
        "sample_index": draw_sample_index(jax.random.fold_in(keys[5], 71), 0),
        "psf": jnp.clip(jnp.exp(jax.random.uniform(keys[3], (V, 3, RANK, TAPS), jnp.float32, math.log(0.05), math.log(1.0))), 0.05, 1.0),
        "estimate": jnp.clip(jnp.exp(math.log(2.0) - 1.3862944 * jax.random.uniform(keys[4], (NZ, NY, NX), jnp.float32) ** shard_levels(keys[4], (NZ, NY, NX), ((0, 4), (1, 8), (2, 8)), -0.2, 0.2)), 0.5, 2.0),
    }


def line_pass(values, kernel, axis_num, length):
    total = kernel[0] * lax.slice_in_dim(values, 0, length, axis=axis_num)
    for tap_idx in range(1, kernel.shape[0]):
        total = total + kernel[tap_idx] * lax.slice_in_dim(values, tap_idx, tap_idx + length, axis=axis_num)
    return total


def blur_valid(padded, kernels, flipped):
    reach = kernels.shape[-1] - 1
    out_z = padded.shape[0] - reach
    out_y = padded.shape[1] - reach
    out_x = padded.shape[2] - reach
    total = None
    for rank_idx in range(kernels.shape[1]):
        kern_z = kernels[0, rank_idx]
        kern_y = kernels[1, rank_idx]
        kern_x = kernels[2, rank_idx]
        if flipped:
            kern_z = kern_z[::-1]
            kern_y = kern_y[::-1]
            kern_x = kern_x[::-1]
        result = line_pass(padded, kern_x, 2, out_x)
        result = line_pass(result, kern_y, 1, out_y)
        result = line_pass(result, kern_z, 0, out_z)
        total = result if total is None else total + result
    return total


def psf_norms(psf):
    return 1.0 / jnp.sum(jnp.prod(jnp.sum(psf, axis=-1), axis=1), axis=-1)


def reference(raw_views, interp_weight, sample_index, psf, estimate):
    views = raw_views.shape[0]
    half = psf.shape[-1] // 2
    data = []
    for view_idx in range(views):
        first_idx = sample_index[view_idx].astype(jnp.int32)
        second_idx = (sample_index[view_idx] + 1).astype(jnp.int32)
        weight_row = interp_weight[view_idx]
        lower = jnp.take(raw_views[view_idx], first_idx, axis=2)
        upper = jnp.take(raw_views[view_idx], second_idx, axis=2)
        data.append((1.0 - weight_row) * lower + weight_row * upper)
    norms = psf_norms(psf)
    current = estimate
    for round_idx in range(ITERS):
        for view_idx in range(views):
            kernels = psf[view_idx]
            blurred = blur_valid(jnp.pad(current, half), kernels, False) * norms[view_idx]
            ratio = data[view_idx] / blurred
            current = current * (blur_valid(jnp.pad(ratio, half), kernels, True) * norms[view_idx])
    return current
```

```python
import jax
import jax.numpy as jnp
from jax import lax
from jax.experimental import pallas as pl
from jax.experimental.pallas import tpu as pltpu
from jax.sharding import PartitionSpec as P

MESH = pl.DeviceIdType.MESH
F32 = jnp.float32
STEPS = (-1, 0, 1)
AROUND = [(dz, dy, dx) for dx in STEPS for dz in STEPS for dy in STEPS if (dz, dy, dx) != (0, 0, 0)]
HALF = 4
TAPS = 9
RANK = 4


def window(ref, slot, dz, dy, arriving):
    planes = {
        0: (4, 8),
        1: (12, 4) if arriving else (8, 4),
        -1: (0, 4) if arriving else (4, 4),
    }[dz]
    rows = {
        0: (8, 16),
        1: (24, 8) if arriving else (16, 8),
        -1: (0, 8) if arriving else (8, 8),
    }[dy]
    return ref.at[slot, pl.ds(*planes), pl.ds(*rows), :]


def kernel(
    sizes,
    psf_ref,
    weight_ref,
    index_ref,
    raw_ref,
    est_ref,
    out_ref,
    field,
    edge_out,
    edge_in,
    mixed,
    after_x,
    after_z,
    beside,
    data,
    send_sem,
    recv_sem,
    raw_send,
    raw_recv,
):
    views = raw_ref.shape[0]
    spots = [lax.axis_index(a) for a in ("gz", "gy", "gx")]
    here = dict(zip(("gz", "gy", "gx"), spots))

    def peer(dz, dy, dx):
        spot = {}
        for axis, by in (("gz", dz), ("gy", dy), ("gx", dx)):
            spot[axis] = lax.rem(here[axis] + (by + sizes[axis]), sizes[axis])
        return spot

    barrier = pltpu.get_barrier_semaphore()
    for offset in AROUND:
        pl.semaphore_signal(barrier, inc=1, device_id=peer(*offset), device_id_type=MESH)

    lane8 = lax.broadcasted_iota(jnp.int32, (8, 128), 1)
    sub8 = lax.broadcasted_iota(jnp.int32, (8, 128), 0)
    lane16 = lax.broadcasted_iota(jnp.int32, (16, 128), 1)
    lane24 = lax.broadcasted_iota(jnp.int32, (24, 128), 1)
    inside = {}
    for axis in ("gz", "gy", "gx"):
        inside[axis] = (
            (here[axis] > 0).astype(jnp.int32),
            (here[axis] < sizes[axis] - 1).astype(jnp.int32),
        )
    from_right8 = (lane8 % 8) >= 4
    rows_ok = jnp.where(sub8 < 4, inside["gy"][1], inside["gy"][0])
    cols_ok = jnp.where(from_right8, inside["gx"][1], inside["gx"][0])

    def packed(pack, plane, num):
        moved = pltpu.roll(plane, 4 + 8 * num, 1)
        return jnp.where(lane16 // 8 == num, moved, pack)

    def halo_copies(slot):
        copies = []
        for num, (dz, dy, dx) in enumerate(AROUND):
            if dx == 0:
                src = window(field, slot, dz, dy, False)
                dst = window(field, slot, -dz, -dy, True)
            else:
                src = edge_out.at[slot]
                dst = edge_in.at[slot, (1 - dx) // 2, 1 - dz, 1 - dy]
            copies.append(
                pltpu.make_async_remote_copy(
                    src_ref=src,
                    dst_ref=dst,
                    send_sem=send_sem.at[slot, num],
                    recv_sem=recv_sem.at[slot, num],
                    device_id=peer(dz, dy, dx),
                    device_id_type=MESH,
                )
            )
        return copies

    def raw_copies(view):
        return [
            pltpu.make_async_remote_copy(
                src_ref=raw_ref.at[view],
                dst_ref=beside.at[side, view],
                send_sem=raw_send.at[side, view],
                recv_sem=raw_recv.at[side, view],
                device_id=peer(0, 0, by),
                device_id_type=MESH,
            )
            for side, by in ((0, 1), (1, -1))
        ]

    def make_data(view):
        for copy in raw_copies(view):
            copy.wait()
        own = pl.ds(pl.multiple_of(here["gx"] * 128, 128), 128)
        row = lax.broadcasted_iota(jnp.int32, (views, 128), 0)
        first = jnp.sum(jnp.where(row == view, index_ref[:, own], 0), axis=0, keepdims=True)
        weight = jnp.sum(jnp.where(row == view, weight_ref[:, own], 0.0), axis=0, keepdims=True)
        source = lax.broadcasted_iota(jnp.int32, (128, 128), 0)
        total = None
        for brick, ref in ((-1, beside.at[0]), (0, raw_ref), (1, beside.at[1])):
            at = source + (here["gx"] + brick) * 128
            table = jnp.where(at == first, 1.0 - weight, 0.0)
            table = table + jnp.where(at == first + 1, weight, 0.0)
            part = jnp.dot(
                ref[view].reshape(128, 128),
                table,
                precision=lax.Precision.HIGHEST,
                preferred_element_type=F32,
            )
            total = part if total is None else total + part
        data[...] = total.reshape(8, 16, 128)

    def taps(view, axis, flipped):
        return [
            [psf_ref[view, axis, r, TAPS - 1 - t if flipped else t] for t in range(TAPS)]
            for r in range(RANK)
        ]

    def norm_of(view):
        total = 0.0
        for r in range(RANK):
            prod = None
            for axis in range(3):
                line = psf_ref[view, axis, r, 0]
                for t in range(1, TAPS):
                    line = line + psf_ref[view, axis, r, t]
                prod = line if prod is None else prod * line
            total = total + prod
        return 1.0 / jnp.full((16, 128), total, F32)

    def blur(slot, view, flipped, use):
        kx = taps(view, 2, flipped)
        for dz in range(3):
            seen = []
            for dy in range(3):
                left, right = edge_in[slot, 0, dz, dy], edge_in[slot, 1, dz, dy]
                both = jnp.where((lane16 % 8) >= 4, right, left)
                cols16 = jnp.concatenate([cols_ok, cols_ok], axis=0)
                seen.append(jnp.where(cols16 > 0, both, 0.0))
            ok = jnp.full((8, 128), (inside["gz"][0], 1, inside["gz"][1])[dz], jnp.int32)
            ok16 = jnp.concatenate([ok, ok], axis=0)
            edge = jnp.where(sub8 < 4, seen[2][0:8], seen[0][8:16])
            mixed[dz, 0:8] = jnp.where(jnp.logical_and(rows_ok > 0, ok > 0), edge, 0.0)
            mixed[dz, 8:24] = jnp.where(ok16 > 0, seen[1], 0.0)

        def x_step(i, carry):
            part = (i + 1) // 2
            ok = jnp.where(i == 0, inside["gz"][0], jnp.where(i == 3, inside["gz"][1], 1))
            ok8 = jnp.full((8, 128), ok, jnp.int32)
            ok16 = jnp.full((16, 128), ok, jnp.int32)
            halo = mixed[part]
            for j in range(4):
                z = i * 4 + j
                edge = jnp.where(sub8 < 4, field[slot, z, 24:32], field[slot, z, 0:8])
                edge = jnp.where(jnp.logical_and(rows_ok > 0, ok8 > 0), edge, 0.0)
                own = jnp.where(ok16 > 0, field[slot, z, 8:24], 0.0)
                here_f = jnp.concatenate([edge, own], axis=0)
                shift = 128 - 4 - 8 * j - 32 * ((i + 1) % 2)
                side = pltpu.roll(halo, shift, 1)
                sums = [None] * RANK
                for t in range(TAPS):
                    s = t - HALF
                    if s == 0:
                        moved = here_f
                    elif s > 0:
                        moved = pltpu.roll(jnp.where(lane24 < s, side, here_f), 128 - s, 1)
                    else:
                        moved = pltpu.roll(jnp.where(lane24 >= 128 + s, side, here_f), -s, 1)
                    for r in range(RANK):
                        term = kx[r][t] * moved
                        sums[r] = term if sums[r] is None else sums[r] + term
                for r in range(RANK):
                    after_x[r, z] = sums[r]
            return carry

        lax.fori_loop(0, 4, x_step, 0)
        kz = taps(view, 0, flipped)

        def z_step(z, carry):
            for r in range(RANK):
                total = kz[r][0] * after_x[r, z]
                for t in range(1, TAPS):
                    total = total + kz[r][t] * after_x[r, z + t]
                after_z[r, z, 0:24] = total
                after_z[r, z, 24:32] = total[0:8]
            return carry

        lax.fori_loop(0, 8, z_step, 0)
        ky = taps(view, 1, flipped)

        def y_step(z, pack):
            total = None
            for r in range(RANK):
                for t in range(TAPS):
                    term = ky[r][t] * after_z[r, z, HALF + t : HALF + t + 16]
                    total = term if total is None else total + term
            plane = use(z, total)
            return packed(pack, plane, z)

        return lax.fori_loop(0, 8, y_step, jnp.zeros((16, 128), F32))

    pack = jnp.zeros((16, 128), F32)
    for z in range(8):
        plane = est_ref[z]
        field[0, 4 + z, 8:24] = plane
        pack = packed(pack, plane, z)
    edge_out[0] = pack

    pl.semaphore_wait(barrier, len(AROUND))

    for copy in halo_copies(0):
        copy.start()
    for view in range(views):
        for copy in raw_copies(view):
            copy.start()

    def view_step(view, carry):
        make_data(view)
        norm = norm_of(view)
        for copy in halo_copies(0):
            copy.wait()

        def to_ratio(z, total):
            plane = data[z] / (total * norm)
            field[1, 4 + z, 8:24] = plane
            return plane

        edge_out[1] = blur(0, view, False, to_ratio)
        for copy in halo_copies(1):
            copy.start()
        for copy in halo_copies(1):
            copy.wait()

        def to_current(z, total):
            plane = field[0, 4 + z, 8:24] * (total * norm)
            field[0, 4 + z, 8:24] = plane
            out_ref[z] = plane
            return plane

        edge_out[0] = blur(1, view, True, to_current)

        @pl.when(view < views - 1)
        def _():
            for copy in halo_copies(0):
                copy.start()

        return carry

    lax.fori_loop(0, views, view_step, 0)


def solution(mesh):
    sizes = dict(mesh.shape)

    def shards(raw_views, interp_weight, sample_index, psf, estimate):
        vmem = pl.BlockSpec(memory_space=pltpu.VMEM)
        smem = pl.BlockSpec(memory_space=pltpu.SMEM)
        num = len(AROUND)
        views = raw_views.shape[0]

        def body(*refs):
            kernel(sizes, *refs)

        return pl.pallas_call(
            body,
            out_shape=jax.ShapeDtypeStruct(estimate.shape, F32),
            in_specs=[smem, vmem, vmem, vmem, vmem],
            out_specs=vmem,
            scratch_shapes=[
                pltpu.VMEM((2, 16, 32, 128), F32),
                pltpu.VMEM((2, 16, 128), F32),
                pltpu.VMEM((2, 2, 3, 3, 16, 128), F32),
                pltpu.VMEM((3, 24, 128), F32),
                pltpu.VMEM((RANK, 16, 24, 128), F32),
                pltpu.VMEM((RANK, 8, 32, 128), F32),
                pltpu.VMEM((2, views, 8, 16, 128), F32),
                pltpu.VMEM((8, 16, 128), F32),
                pltpu.SemaphoreType.DMA((2, num)),
                pltpu.SemaphoreType.DMA((2, num)),
                pltpu.SemaphoreType.DMA((2, views)),
                pltpu.SemaphoreType.DMA((2, views)),
            ],
            compiler_params=pltpu.CompilerParams(collective_id=0, has_side_effects=True),
            name="deconvolve",
        )(psf, interp_weight, sample_index, raw_views, estimate)

    return jax.shard_map(
        shards,
        mesh=mesh,
        in_specs=(P(None, "gz", "gy", "gx"), P(), P(), P(), P("gz", "gy", "gx")),
        out_specs=P("gz", "gy", "gx"),
        check_vma=False,
    )
```

```python
import jax
import jax.numpy as jnp
from jax import lax
from jax.experimental import pallas as pl
from jax.experimental.pallas import tpu as pltpu
from jax.sharding import PartitionSpec as P

MESH = pl.DeviceIdType.MESH
F32 = jnp.float32
STEPS = (-1, 0, 1)
AROUND = [(dz, dy, dx) for dx in STEPS for dz in STEPS for dy in STEPS if (dz, dy, dx) != (0, 0, 0)]
HALF = 4
TAPS = 9
RANK = 4


def window(ref, slot, dz, dy, arriving):
    planes = {
        0: (4, 8),
        1: (12, 4) if arriving else (8, 4),
        -1: (0, 4) if arriving else (4, 4),
    }[dz]
    rows = {
        0: (8, 16),
        1: (24, 4) if arriving else (20, 4),
        -1: (4, 4) if arriving else (8, 4),
    }[dy]
    return ref.at[slot, pl.ds(*planes), pl.ds(*rows), :]


def kernel(
    sizes,
    psf_ref,
    weight_ref,
    index_ref,
    raw_ref,
    est_ref,
    out_ref,
    field,
    edge_out,
    edge_in,
    mixed,
    after_x,
    after_z,
    beside,
    data,
    send_sem,
    recv_sem,
    raw_send,
    raw_recv,
):
    views = raw_ref.shape[0]
    spots = [lax.axis_index(a) for a in ("gz", "gy", "gx")]
    here = dict(zip(("gz", "gy", "gx"), spots))

    def peer(dz, dy, dx):
        spot = {}
        for axis, by in (("gz", dz), ("gy", dy), ("gx", dx)):
            spot[axis] = lax.rem(here[axis] + (by + sizes[axis]), sizes[axis])
        return spot

    barrier = pltpu.get_barrier_semaphore()
    for offset in AROUND:
        pl.semaphore_signal(barrier, inc=1, device_id=peer(*offset), device_id_type=MESH)

    lane8 = lax.broadcasted_iota(jnp.int32, (8, 128), 1)
    sub8 = lax.broadcasted_iota(jnp.int32, (8, 128), 0)
    lane16 = lax.broadcasted_iota(jnp.int32, (16, 128), 1)
    lane24 = lax.broadcasted_iota(jnp.int32, (24, 128), 1)
    inside = {}
    for axis in ("gz", "gy", "gx"):
        inside[axis] = (
            (here[axis] > 0).astype(jnp.int32),
            (here[axis] < sizes[axis] - 1).astype(jnp.int32),
        )
    from_right8 = (lane8 % 8) >= 4
    rows_ok = jnp.where(sub8 < 4, inside["gy"][1], inside["gy"][0])
    cols_ok = jnp.where(from_right8, inside["gx"][1], inside["gx"][0])

    def packed(pack, plane, num):
        moved = pltpu.roll(plane, 4 + 8 * num, 1)
        return jnp.where(lane16 // 8 == num, moved, pack)

    def halo_copies(slot):
        copies = []
        for num, (dz, dy, dx) in enumerate(AROUND):
            if dx == 0:
                src = window(field, slot, dz, dy, False)
                dst = window(field, slot, -dz, -dy, True)
            else:
                rows = pl.ds(*{0: (0, 16), 1: (12, 4), -1: (0, 4)}[dy])
                src = edge_out.at[slot, rows]
                dst = edge_in.at[slot, (1 - dx) // 2, 1 - dz, 1 - dy, rows]
            copies.append(
                pltpu.make_async_remote_copy(
                    src_ref=src,
                    dst_ref=dst,
                    send_sem=send_sem.at[slot, num],
                    recv_sem=recv_sem.at[slot, num],
                    device_id=peer(dz, dy, dx),
                    device_id_type=MESH,
                )
            )
        return copies

    def raw_copies(view):
        return [
            pltpu.make_async_remote_copy(
                src_ref=raw_ref.at[view],
                dst_ref=beside.at[side, view],
                send_sem=raw_send.at[side, view],
                recv_sem=raw_recv.at[side, view],
                device_id=peer(0, 0, by),
                device_id_type=MESH,
            )
            for side, by in ((0, 1), (1, -1))
        ]

    def make_data(view):
        for copy in raw_copies(view):
            copy.wait()
        own = pl.ds(pl.multiple_of(here["gx"] * 128, 128), 128)
        row = lax.broadcasted_iota(jnp.int32, (views, 128), 0)
        first = jnp.sum(jnp.where(row == view, index_ref[:, own], 0), axis=0, keepdims=True)
        weight = jnp.sum(jnp.where(row == view, weight_ref[:, own], 0.0), axis=0, keepdims=True)
        source = lax.broadcasted_iota(jnp.int32, (128, 128), 0)
        total = None
        for brick, ref in ((-1, beside.at[0]), (0, raw_ref), (1, beside.at[1])):
            at = source + (here["gx"] + brick) * 128
            table = jnp.where(at == first, 1.0 - weight, 0.0)
            table = table + jnp.where(at == first + 1, weight, 0.0)
            part = jnp.dot(
                ref[view].reshape(128, 128),
                table,
                precision=lax.Precision.HIGHEST,
                preferred_element_type=F32,
            )
            total = part if total is None else total + part
        data[...] = total.reshape(8, 16, 128)

    def taps(view, axis, flipped):
        return [
            [psf_ref[view, axis, r, TAPS - 1 - t if flipped else t] for t in range(TAPS)]
            for r in range(RANK)
        ]

    def norm_of(view):
        total = 0.0
        for r in range(RANK):
            prod = None
            for axis in range(3):
                line = psf_ref[view, axis, r, 0]
                for t in range(1, TAPS):
                    line = line + psf_ref[view, axis, r, t]
                prod = line if prod is None else prod * line
            total = total + prod
        return 1.0 / jnp.full((16, 128), total, F32)

    def blur(slot, view, flipped, use):
        kx = taps(view, 2, flipped)
        for dz in range(3):
            seen = []
            for dy in range(3):
                left, right = edge_in[slot, 0, dz, dy], edge_in[slot, 1, dz, dy]
                both = jnp.where((lane16 % 8) >= 4, right, left)
                cols16 = jnp.concatenate([cols_ok, cols_ok], axis=0)
                seen.append(jnp.where(cols16 > 0, both, 0.0))
            ok = jnp.full((8, 128), (inside["gz"][0], 1, inside["gz"][1])[dz], jnp.int32)
            ok16 = jnp.concatenate([ok, ok], axis=0)
            edge = jnp.where(sub8 < 4, seen[2][0:8], seen[0][8:16])
            mixed[dz, 0:8] = jnp.where(jnp.logical_and(rows_ok > 0, ok > 0), edge, 0.0)
            mixed[dz, 8:24] = jnp.where(ok16 > 0, seen[1], 0.0)

        def x_step(i, carry):
            part = (i + 1) // 2
            ok = jnp.where(i == 0, inside["gz"][0], jnp.where(i == 3, inside["gz"][1], 1))
            ok8 = jnp.full((8, 128), ok, jnp.int32)
            ok16 = jnp.full((16, 128), ok, jnp.int32)
            halo = mixed[part]
            for j in range(4):
                z = i * 4 + j
                edge = jnp.where(sub8 < 4, field[slot, z, 24:32], field[slot, z, 0:8])
                edge = jnp.where(jnp.logical_and(rows_ok > 0, ok8 > 0), edge, 0.0)
                own = jnp.where(ok16 > 0, field[slot, z, 8:24], 0.0)
                here_f = jnp.concatenate([edge, own], axis=0)
                shift = 128 - 4 - 8 * j - 32 * ((i + 1) % 2)
                side = pltpu.roll(halo, shift, 1)
                sums = [None] * RANK
                for t in range(TAPS):
                    s = t - HALF
                    if s == 0:
                        moved = here_f
                    elif s > 0:
                        moved = pltpu.roll(jnp.where(lane24 < s, side, here_f), 128 - s, 1)
                    else:
                        moved = pltpu.roll(jnp.where(lane24 >= 128 + s, side, here_f), -s, 1)
                    for r in range(RANK):
                        term = kx[r][t] * moved
                        sums[r] = term if sums[r] is None else sums[r] + term
                for r in range(RANK):
                    after_x[r, z] = sums[r]
            return carry

        lax.fori_loop(0, 4, x_step, 0)
        kz = taps(view, 0, flipped)

        def z_step(z, carry):
            for r in range(RANK):
                total = kz[r][0] * after_x[r, z]
                for t in range(1, TAPS):
                    total = total + kz[r][t] * after_x[r, z + t]
                after_z[r, z, 0:24] = total
                after_z[r, z, 24:32] = total[0:8]
            return carry

        lax.fori_loop(0, 8, z_step, 0)
        ky = taps(view, 1, flipped)

        def y_step(z, pack):
            total = None
            for r in range(RANK):
                for t in range(TAPS):
                    term = ky[r][t] * after_z[r, z, HALF + t : HALF + t + 16]
                    total = term if total is None else total + term
            plane = use(z, total)
            return packed(pack, plane, z)

        return lax.fori_loop(0, 8, y_step, jnp.zeros((16, 128), F32))

    pack = jnp.zeros((16, 128), F32)
    for z in range(8):
        plane = est_ref[z]
        field[0, 4 + z, 8:24] = plane
        pack = packed(pack, plane, z)
    edge_out[0] = pack

    pl.semaphore_wait(barrier, len(AROUND))

    for copy in halo_copies(0):
        copy.start()
    for view in range(views):
        for copy in raw_copies(view):
            copy.start()

    def view_step(view, carry):
        make_data(view)
        norm = norm_of(view)
        for copy in halo_copies(0):
            copy.wait()

        def to_ratio(z, total):
            plane = data[z] / (total * norm)
            field[1, 4 + z, 8:24] = plane
            return plane

        edge_out[1] = blur(0, view, False, to_ratio)
        for copy in halo_copies(1):
            copy.start()
        for copy in halo_copies(1):
            copy.wait()

        def to_current(z, total):
            plane = field[0, 4 + z, 8:24] * (total * norm)
            field[0, 4 + z, 8:24] = plane
            out_ref[z] = plane
            return plane

        edge_out[0] = blur(1, view, True, to_current)

        @pl.when(view < views - 1)
        def _():
            for copy in halo_copies(0):
                copy.start()

        return carry

    lax.fori_loop(0, views, view_step, 0)


def solution(mesh):
    sizes = dict(mesh.shape)

    def shards(raw_views, interp_weight, sample_index, psf, estimate):
        vmem = pl.BlockSpec(memory_space=pltpu.VMEM)
        smem = pl.BlockSpec(memory_space=pltpu.SMEM)
        num = len(AROUND)
        views = raw_views.shape[0]

        def body(*refs):
            kernel(sizes, *refs)

        return pl.pallas_call(
            body,
            out_shape=jax.ShapeDtypeStruct(estimate.shape, F32),
            in_specs=[smem, vmem, vmem, vmem, vmem],
            out_specs=vmem,
            scratch_shapes=[
                pltpu.VMEM((2, 16, 32, 128), F32),
                pltpu.VMEM((2, 16, 128), F32),
                pltpu.VMEM((2, 2, 3, 3, 16, 128), F32),
                pltpu.VMEM((3, 24, 128), F32),
                pltpu.VMEM((RANK, 16, 24, 128), F32),
                pltpu.VMEM((RANK, 8, 32, 128), F32),
                pltpu.VMEM((2, views, 8, 16, 128), F32),
                pltpu.VMEM((8, 16, 128), F32),
                pltpu.SemaphoreType.DMA((2, num)),
                pltpu.SemaphoreType.DMA((2, num)),
                pltpu.SemaphoreType.DMA((2, views)),
                pltpu.SemaphoreType.DMA((2, views)),
            ],
            compiler_params=pltpu.CompilerParams(collective_id=0, has_side_effects=True),
            name="deconvolve",
        )(psf, interp_weight, sample_index, raw_views, estimate)

    return jax.shard_map(
        shards,
        mesh=mesh,
        in_specs=(P(None, "gz", "gy", "gx"), P(), P(), P(), P("gz", "gy", "gx")),
        out_specs=P("gz", "gy", "gx"),
        check_vma=False,
    )
```

```python
import jax
import jax.numpy as jnp
from jax import lax
from jax.experimental import pallas as pl
from jax.experimental.pallas import tpu as pltpu
from jax.sharding import PartitionSpec as P

MESH = pl.DeviceIdType.MESH
F32 = jnp.float32
STEPS = (-1, 0, 1)
AROUND = [(dz, dy, dx) for dx in STEPS for dz in STEPS for dy in STEPS if (dz, dy, dx) != (0, 0, 0)]
HALF = 4
TAPS = 9
RANK = 4


def window(ref, slot, dz, dy, arriving):
    planes = {
        0: (4, 8),
        1: (12, 4) if arriving else (8, 4),
        -1: (0, 4) if arriving else (4, 4),
    }[dz]
    rows = {
        0: (8, 16),
        1: (24, 4) if arriving else (20, 4),
        -1: (4, 4) if arriving else (8, 4),
    }[dy]
    return ref.at[slot, pl.ds(*planes), pl.ds(*rows), :]


def kernel(
    sizes,
    psf_ref,
    weight_ref,
    index_ref,
    raw_ref,
    est_ref,
    out_ref,
    field,
    edge_out,
    edge_in,
    part,
    after_x,
    after_z,
    beside,
    data,
    send_sem,
    recv_sem,
    raw_send,
    raw_recv,
):
    views = raw_ref.shape[0]
    spots = [lax.axis_index(a) for a in ("gz", "gy", "gx")]
    here = dict(zip(("gz", "gy", "gx"), spots))

    def peer(dz, dy, dx):
        spot = {}
        for axis, by in (("gz", dz), ("gy", dy), ("gx", dx)):
            spot[axis] = lax.rem(here[axis] + (by + sizes[axis]), sizes[axis])
        return spot

    barrier = pltpu.get_barrier_semaphore()
    for offset in AROUND:
        pl.semaphore_signal(barrier, inc=1, device_id=peer(*offset), device_id_type=MESH)

    lane8 = lax.broadcasted_iota(jnp.int32, (8, 128), 1)
    sub8 = lax.broadcasted_iota(jnp.int32, (8, 128), 0)
    lane16 = lax.broadcasted_iota(jnp.int32, (16, 128), 1)
    lane24 = lax.broadcasted_iota(jnp.int32, (24, 128), 1)
    inside = {}
    for axis in ("gz", "gy", "gx"):
        inside[axis] = (
            (here[axis] > 0).astype(jnp.int32),
            (here[axis] < sizes[axis] - 1).astype(jnp.int32),
        )
    from_right8 = (lane8 % 8) >= 4
    rows_ok = jnp.where(sub8 < 4, inside["gy"][1], inside["gy"][0])
    cols_ok = jnp.where(from_right8, inside["gx"][1], inside["gx"][0])

    def packed(pack, plane, num):
        moved = pltpu.roll(plane, 4 + 8 * num, 1)
        return jnp.where(lane16 // 8 == num, moved, pack)

    peers = {offset: peer(*offset) for offset in AROUND}

    def send_halos(slot):
        for dz, dy, dx in AROUND:
            if dx == 0:
                src = window(field, slot, dz, dy, False)
                dst = window(field, slot, -dz, -dy, True)
            else:
                rows = pl.ds(*{0: (0, 16), 1: (12, 4), -1: (0, 4)}[dy])
                src = edge_out.at[slot, rows]
                dst = edge_in.at[slot, (1 - dx) // 2, 1 - dz, 1 - dy, rows]
            kind = 0 if dx == 0 else 1
            pltpu.make_async_remote_copy(
                src_ref=src,
                dst_ref=dst,
                send_sem=send_sem.at[slot, kind],
                recv_sem=recv_sem.at[slot, kind],
                device_id=peers[dz, dy, dx],
                device_id_type=MESH,
            ).start()

    def wait_halos(slot, kind, sem):
        whole = field.at[slot, :, pl.ds(0, 16), :] if kind == 0 else edge_in.at[slot, 0]
        pltpu.make_async_copy(whole, whole, sem.at[slot, kind]).wait()

    def raw_copies(view):
        return [
            pltpu.make_async_remote_copy(
                src_ref=raw_ref.at[view],
                dst_ref=beside.at[side, view],
                send_sem=raw_send.at[side, view],
                recv_sem=raw_recv.at[side, view],
                device_id=peer(0, 0, by),
                device_id_type=MESH,
            )
            for side, by in ((0, 1), (1, -1))
        ]

    def make_data(view):
        for copy in raw_copies(view):
            copy.wait()
        own = pl.ds(pl.multiple_of(here["gx"] * 128, 128), 128)
        row = lax.broadcasted_iota(jnp.int32, (views, 128), 0)
        first = jnp.sum(jnp.where(row == view, index_ref[:, own], 0), axis=0, keepdims=True)
        weight = jnp.sum(jnp.where(row == view, weight_ref[:, own], 0.0), axis=0, keepdims=True)
        source = lax.broadcasted_iota(jnp.int32, (128, 128), 0)
        total = None
        for brick, ref in ((-1, beside.at[0]), (0, raw_ref), (1, beside.at[1])):
            at = source + (here["gx"] + brick) * 128
            table = jnp.where(at == first, 1.0 - weight, 0.0)
            table = table + jnp.where(at == first + 1, weight, 0.0)
            part = jnp.dot(
                ref[view].reshape(128, 128),
                table,
                precision=lax.Precision.HIGHEST,
                preferred_element_type=F32,
            )
            total = part if total is None else total + part
        data[...] = total.reshape(8, 16, 128)

    def taps(view, axis, flipped):
        return [
            [psf_ref[view, axis, r, TAPS - 1 - t if flipped else t] for t in range(TAPS)]
            for r in range(RANK)
        ]

    def norm_of(view):
        total = 0.0
        for r in range(RANK):
            prod = None
            for axis in range(3):
                line = psf_ref[view, axis, r, 0]
                for t in range(1, TAPS):
                    line = line + psf_ref[view, axis, r, t]
                prod = line if prod is None else prod * line
            total = total + prod
        return 1.0 / jnp.full((16, 128), total, F32)

    def x_lines(lines, kx, store):
        lane = lax.broadcasted_iota(jnp.int32, lines.shape, 1)
        sums = [None] * RANK
        for t in range(TAPS):
            s = t - HALF
            if s == 0:
                moved = lines
            elif s > 0:
                moved = pltpu.roll(jnp.where(lane < s, 0.0, lines), 128 - s, 1)
            else:
                moved = pltpu.roll(jnp.where(lane >= 128 + s, 0.0, lines), -s, 1)
            for r in range(RANK):
                term = kx[r][t] * moved
                sums[r] = term if sums[r] is None else sums[r] + term
        for r in range(RANK):
            store(r, sums[r])

    def y_lines(ky, z):
        total = None
        for r in range(RANK):
            for t in range(TAPS):
                term = ky[r][t] * after_z[r, z, HALF + t : HALF + t + 16]
                total = term if total is None else total + term
        return total

    def edge_rows(slot, z, ok):
        edge = jnp.where(sub8 < 4, field[slot, z, 24:32], field[slot, z, 0:8])
        return jnp.where(jnp.logical_and(rows_ok > 0, ok > 0), edge, 0.0)

    def blur(slot, view, flipped, use, meanwhile):
        kz, ky, kx = [taps(view, axis, flipped) for axis in range(3)]

        def own_step(i, carry):
            for j in range(4):
                z = 4 + i * 4 + j

                def store(r, value):
                    after_x[r, z, 8:24] = value

                x_lines(field[slot, z, 8:24], kx, store)
            return carry

        lax.fori_loop(0, 2, own_step, 0)
        meanwhile()
        wait_halos(slot, 0, recv_sem)

        def far_step(i, carry):
            ok = jnp.where(i == 0, inside["gz"][0], inside["gz"][1])
            ok8 = jnp.full((8, 128), ok, jnp.int32)
            ok16 = jnp.full((16, 128), ok, jnp.int32)
            for j in range(4):
                z = 12 * i + j
                own = jnp.where(ok16 > 0, field[slot, z, 8:24], 0.0)
                lines = jnp.concatenate([edge_rows(slot, z, ok8), own], axis=0)

                def store(r, value):
                    after_x[r, z] = value

                x_lines(lines, kx, store)
            return carry

        lax.fori_loop(0, 2, far_step, 0)
        always = jnp.full((8, 128), 1, jnp.int32)

        def near_step(i, carry):
            for j in range(4):
                z = 4 + i * 4 + j

                def store(r, value):
                    after_x[r, z, 0:8] = value

                x_lines(edge_rows(slot, z, always), kx, store)
            return carry

        lax.fori_loop(0, 2, near_step, 0)

        def z_step(z, carry):
            for r in range(RANK):
                total = kz[r][0] * after_x[r, z]
                for t in range(1, TAPS):
                    total = total + kz[r][t] * after_x[r, z + t]
                after_z[r, z, 0:24] = total
                after_z[r, z, 24:32] = total[0:8]
            return carry

        lax.fori_loop(0, 8, z_step, 0)

        def y_step(z, carry):
            part[z] = y_lines(ky, z)
            return carry

        lax.fori_loop(0, 8, y_step, 0)
        wait_halos(slot, 1, recv_sem)
        wait_halos(slot, 0, send_sem)
        wait_halos(slot, 1, send_sem)

        groups = []
        for dz in range(3):
            seen = []
            for dy in range(3):
                left, right = edge_in[slot, 0, dz, dy], edge_in[slot, 1, dz, dy]
                seen.append(jnp.where((lane16 % 8) >= 4, right, left))
            ok = (inside["gz"][0], 1, inside["gz"][1])[dz]
            ok8 = jnp.logical_and(jnp.full((8, 128), ok, jnp.int32) > 0, cols_ok > 0)
            edge = jnp.where(sub8 < 4, seen[2][0:8], seen[0][8:16])
            edge = jnp.where(jnp.logical_and(rows_ok > 0, ok8), edge, 0.0)
            rows = [edge] + [jnp.where(ok8, seen[1][8 * h : 8 * h + 8], 0.0) for h in range(2)]
            groups.append(pltpu.roll(jnp.concatenate(rows, axis=0), (96, 32, 96)[dz], 1))
        lines = jnp.where(lane24 < 32, groups[0], jnp.where(lane24 < 96, groups[1], groups[2]))
        moved = [pltpu.roll(lines, (8 * (HALF - t)) % 128, 1) if t != HALF else lines for t in range(TAPS)]
        spot24 = lane24 % 8
        for r in range(RANK):
            over_z = None
            for t in range(TAPS):
                term = kz[r][t] * moved[t]
                over_z = term if over_z is None else over_z + term
            total = None
            for d in range(HALF):
                below = pltpu.roll(over_z, 128 - d, 1) if d else over_z
                above = pltpu.roll(over_z, d, 1) if d else over_z
                below = jnp.where(spot24 + d <= 3, below, 0.0)
                above = jnp.where(spot24 - d >= 4, above, 0.0)
                term = kx[r][d] * below + kx[r][TAPS - 1 - d] * above
                total = term if total is None else total + term
            after_z[r, 0, 0:24] = total
            after_z[r, 0, 24:32] = total[0:8]
        beyond = y_lines(ky, 0)
        beyond = jnp.where((lane16 % 8) < 4, pltpu.roll(beyond, 124, 1), pltpu.roll(beyond, 4, 1))
        at_edge = jnp.logical_or(lane16 < 4, lane16 >= 124)
        pack = jnp.zeros((16, 128), F32)
        for z in range(8):
            add = pltpu.roll(beyond, 128 - (8 * (z + 4) + 4), 1)
            plane = use(z, part[z] + jnp.where(at_edge, add, 0.0))
            pack = packed(pack, plane, z)
        return pack

    pack = jnp.zeros((16, 128), F32)
    for z in range(8):
        plane = est_ref[z]
        field[0, 4 + z, 8:24] = plane
        pack = packed(pack, plane, z)
    edge_out[0] = pack

    pl.semaphore_wait(barrier, len(AROUND))

    send_halos(0)
    for view in range(views):
        for copy in raw_copies(view):
            copy.start()

    def view_step(view, carry):
        norm = norm_of(view)

        def to_ratio(z, total):
            plane = data[z] / (total * norm)
            field[1, 4 + z, 8:24] = plane
            return plane

        edge_out[1] = blur(0, view, False, to_ratio, lambda: make_data(view))
        send_halos(1)

        def to_current(z, total):
            plane = field[0, 4 + z, 8:24] * (total * norm)
            field[0, 4 + z, 8:24] = plane
            out_ref[z] = plane
            return plane

        edge_out[0] = blur(1, view, True, to_current, lambda: None)

        @pl.when(view < views - 1)
        def _():
            send_halos(0)

        return carry

    lax.fori_loop(0, views, view_step, 0)


def solution(mesh):
    sizes = dict(mesh.shape)

    def shards(raw_views, interp_weight, sample_index, psf, estimate):
        vmem = pl.BlockSpec(memory_space=pltpu.VMEM)
        smem = pl.BlockSpec(memory_space=pltpu.SMEM)
        views = raw_views.shape[0]

        def body(*refs):
            kernel(sizes, *refs)

        return pl.pallas_call(
            body,
            out_shape=jax.ShapeDtypeStruct(estimate.shape, F32),
            in_specs=[smem, vmem, vmem, vmem, vmem],
            out_specs=vmem,
            scratch_shapes=[
                pltpu.VMEM((2, 16, 32, 128), F32),
                pltpu.VMEM((2, 16, 128), F32),
                pltpu.VMEM((2, 2, 3, 3, 16, 128), F32),
                pltpu.VMEM((8, 16, 128), F32),
                pltpu.VMEM((RANK, 16, 24, 128), F32),
                pltpu.VMEM((RANK, 8, 32, 128), F32),
                pltpu.VMEM((2, views, 8, 16, 128), F32),
                pltpu.VMEM((8, 16, 128), F32),
                pltpu.SemaphoreType.DMA((2, 2)),
                pltpu.SemaphoreType.DMA((2, 2)),
                pltpu.SemaphoreType.DMA((2, views)),
                pltpu.SemaphoreType.DMA((2, views)),
            ],
            compiler_params=pltpu.CompilerParams(collective_id=0, has_side_effects=True),
            name="deconvolve",
        )(psf, interp_weight, sample_index, raw_views, estimate)

    return jax.shard_map(
        shards,
        mesh=mesh,
        in_specs=(P(None, "gz", "gy", "gx"), P(), P(), P(), P("gz", "gy", "gx")),
        out_specs=P("gz", "gy", "gx"),
        check_vma=False,
    )
```

```python
import jax
import jax.numpy as jnp
from jax import lax
from jax.experimental import pallas as pl
from jax.experimental.pallas import tpu as pltpu
from jax.sharding import PartitionSpec as P

MESH = pl.DeviceIdType.MESH
F32 = jnp.float32
STEPS = (-1, 0, 1)
AROUND = [(dz, dy, dx) for dx in STEPS for dz in STEPS for dy in STEPS if (dz, dy, dx) != (0, 0, 0)]
AROUND.sort(key=lambda o: (o[2] != 0, -abs(o[0]) - abs(o[1])))
HALF = 4
TAPS = 9
RANK = 4


def window(ref, slot, dz, dy, arriving):
    planes = {
        0: (4, 8),
        1: (12, 4) if arriving else (8, 4),
        -1: (0, 4) if arriving else (4, 4),
    }[dz]
    rows = {
        0: (8, 16),
        1: (24, 4) if arriving else (20, 4),
        -1: (4, 4) if arriving else (8, 4),
    }[dy]
    return ref.at[slot, pl.ds(*planes), pl.ds(*rows), :]


def kernel(
    sizes,
    psf_ref,
    weight_ref,
    index_ref,
    raw_ref,
    est_ref,
    out_ref,
    field,
    edge_out,
    edge_in,
    part,
    after_x,
    after_z,
    beside,
    data,
    send_sem,
    recv_sem,
    raw_send,
    raw_recv,
):
    views = raw_ref.shape[0]
    spots = [lax.axis_index(a) for a in ("gz", "gy", "gx")]
    here = dict(zip(("gz", "gy", "gx"), spots))

    def peer(dz, dy, dx):
        spot = {}
        for axis, by in (("gz", dz), ("gy", dy), ("gx", dx)):
            spot[axis] = lax.rem(here[axis] + (by + sizes[axis]), sizes[axis])
        return spot

    barrier = pltpu.get_barrier_semaphore()
    for offset in AROUND:
        pl.semaphore_signal(barrier, inc=1, device_id=peer(*offset), device_id_type=MESH)

    lane8 = lax.broadcasted_iota(jnp.int32, (8, 128), 1)
    sub8 = lax.broadcasted_iota(jnp.int32, (8, 128), 0)
    lane16 = lax.broadcasted_iota(jnp.int32, (16, 128), 1)
    lane24 = lax.broadcasted_iota(jnp.int32, (24, 128), 1)
    inside = {}
    for axis in ("gz", "gy", "gx"):
        inside[axis] = (
            (here[axis] > 0).astype(jnp.int32),
            (here[axis] < sizes[axis] - 1).astype(jnp.int32),
        )
    from_right8 = (lane8 % 8) >= 4
    rows_ok = jnp.where(sub8 < 4, inside["gy"][1], inside["gy"][0])
    cols_ok = jnp.where(from_right8, inside["gx"][1], inside["gx"][0])

    def packed(pack, plane, num):
        moved = pltpu.roll(plane, 4 + 8 * num, 1)
        return jnp.where(lane16 // 8 == num, moved, pack)

    peers = {offset: peer(*offset) for offset in AROUND}

    def send_halos(slot):
        for dz, dy, dx in AROUND:
            if dx == 0:
                src = window(field, slot, dz, dy, False)
                dst = window(field, slot, -dz, -dy, True)
            else:
                rows = pl.ds(*{0: (0, 16), 1: (12, 4), -1: (0, 4)}[dy])
                src = edge_out.at[slot, rows]
                dst = edge_in.at[slot, (1 - dx) // 2, 1 - dz, 1 - dy, rows]
            kind = 0 if dx == 0 else 1
            pltpu.make_async_remote_copy(
                src_ref=src,
                dst_ref=dst,
                send_sem=send_sem.at[slot, kind],
                recv_sem=recv_sem.at[slot, kind],
                device_id=peers[dz, dy, dx],
                device_id_type=MESH,
            ).start()

    def wait_halos(slot, kind, sem):
        whole = field.at[slot, :, pl.ds(0, 16), :] if kind == 0 else edge_in.at[slot, 0]
        pltpu.make_async_copy(whole, whole, sem.at[slot, kind]).wait()

    def raw_copies(view):
        return [
            pltpu.make_async_remote_copy(
                src_ref=raw_ref.at[view],
                dst_ref=beside.at[side, view],
                send_sem=raw_send.at[side, view],
                recv_sem=raw_recv.at[side, view],
                device_id=peer(0, 0, by),
                device_id_type=MESH,
            )
            for side, by in ((0, 1), (1, -1))
        ]

    def make_data(view):
        for copy in raw_copies(view):
            copy.wait()
        own = pl.ds(pl.multiple_of(here["gx"] * 128, 128), 128)
        row = lax.broadcasted_iota(jnp.int32, (views, 128), 0)
        first = jnp.sum(jnp.where(row == view, index_ref[:, own], 0), axis=0, keepdims=True)
        weight = jnp.sum(jnp.where(row == view, weight_ref[:, own], 0.0), axis=0, keepdims=True)
        source = lax.broadcasted_iota(jnp.int32, (128, 128), 0)
        total = None
        for brick, ref in ((-1, beside.at[0]), (0, raw_ref), (1, beside.at[1])):
            at = source + (here["gx"] + brick) * 128
            table = jnp.where(at == first, 1.0 - weight, 0.0)
            table = table + jnp.where(at == first + 1, weight, 0.0)
            part = jnp.dot(
                ref[view].reshape(128, 128),
                table,
                precision=lax.Precision.HIGHEST,
                preferred_element_type=F32,
            )
            total = part if total is None else total + part
        data[...] = total.reshape(8, 16, 128)

    def taps(view, axis, flipped):
        return [
            [psf_ref[view, axis, r, TAPS - 1 - t if flipped else t] for t in range(TAPS)]
            for r in range(RANK)
        ]

    def norm_of(view):
        total = 0.0
        for r in range(RANK):
            prod = None
            for axis in range(3):
                line = psf_ref[view, axis, r, 0]
                for t in range(1, TAPS):
                    line = line + psf_ref[view, axis, r, t]
                prod = line if prod is None else prod * line
            total = total + prod
        return 1.0 / jnp.full((16, 128), total, F32)

    def x_lines(lines, kx, store):
        lane = lax.broadcasted_iota(jnp.int32, lines.shape, 1)
        sums = [None] * RANK
        for t in range(TAPS):
            s = t - HALF
            if s == 0:
                moved = lines
            elif s > 0:
                moved = pltpu.roll(jnp.where(lane < s, 0.0, lines), 128 - s, 1)
            else:
                moved = pltpu.roll(jnp.where(lane >= 128 + s, 0.0, lines), -s, 1)
            for r in range(RANK):
                term = kx[r][t] * moved
                sums[r] = term if sums[r] is None else sums[r] + term
        for r in range(RANK):
            store(r, sums[r])

    def y_lines(ky, z):
        total = None
        for r in range(RANK):
            for t in range(TAPS):
                term = ky[r][t] * after_z[r, z, HALF + t : HALF + t + 16]
                total = term if total is None else total + term
        return total

    def edge_rows(slot, z, ok):
        edge = jnp.where(sub8 < 4, field[slot, z, 24:32], field[slot, z, 0:8])
        return jnp.where(jnp.logical_and(rows_ok > 0, ok > 0), edge, 0.0)

    def blur(slot, view, flipped, use, meanwhile):
        kz, ky, kx = [taps(view, axis, flipped) for axis in range(3)]

        def own_step(i, carry):
            for j in range(4):
                z = 4 + i * 4 + j

                def store(r, value):
                    after_x[r, z, 8:24] = value

                x_lines(field[slot, z, 8:24], kx, store)
            return carry

        lax.fori_loop(0, 2, own_step, 0)
        meanwhile()
        wait_halos(slot, 0, recv_sem)

        def far_step(i, carry):
            ok = jnp.where(i == 0, inside["gz"][0], inside["gz"][1])
            ok8 = jnp.full((8, 128), ok, jnp.int32)
            ok16 = jnp.full((16, 128), ok, jnp.int32)
            for j in range(4):
                z = 12 * i + j
                own = jnp.where(ok16 > 0, field[slot, z, 8:24], 0.0)
                lines = jnp.concatenate([edge_rows(slot, z, ok8), own], axis=0)

                def store(r, value):
                    after_x[r, z] = value

                x_lines(lines, kx, store)
            return carry

        lax.fori_loop(0, 2, far_step, 0)
        always = jnp.full((8, 128), 1, jnp.int32)

        def near_step(i, carry):
            for j in range(4):
                z = 4 + i * 4 + j

                def store(r, value):
                    after_x[r, z, 0:8] = value

                x_lines(edge_rows(slot, z, always), kx, store)
            return carry

        lax.fori_loop(0, 2, near_step, 0)

        def z_step(z, carry):
            for r in range(RANK):
                total = kz[r][0] * after_x[r, z]
                for t in range(1, TAPS):
                    total = total + kz[r][t] * after_x[r, z + t]
                after_z[r, z, 0:24] = total
                after_z[r, z, 24:32] = total[0:8]
            return carry

        lax.fori_loop(0, 8, z_step, 0, unroll=2)

        def y_step(z, carry):
            part[z] = y_lines(ky, z)
            return carry

        lax.fori_loop(0, 8, y_step, 0, unroll=4)
        wait_halos(slot, 1, recv_sem)
        wait_halos(slot, 0, send_sem)
        wait_halos(slot, 1, send_sem)

        groups = []
        for dz in range(3):
            seen = []
            for dy in range(3):
                left, right = edge_in[slot, 0, dz, dy], edge_in[slot, 1, dz, dy]
                seen.append(jnp.where((lane16 % 8) >= 4, right, left))
            ok = (inside["gz"][0], 1, inside["gz"][1])[dz]
            ok8 = jnp.logical_and(jnp.full((8, 128), ok, jnp.int32) > 0, cols_ok > 0)
            edge = jnp.where(sub8 < 4, seen[2][0:8], seen[0][8:16])
            edge = jnp.where(jnp.logical_and(rows_ok > 0, ok8), edge, 0.0)
            rows = [edge] + [jnp.where(ok8, seen[1][8 * h : 8 * h + 8], 0.0) for h in range(2)]
            groups.append(pltpu.roll(jnp.concatenate(rows, axis=0), (96, 32, 96)[dz], 1))
        lines = jnp.where(lane24 < 32, groups[0], jnp.where(lane24 < 96, groups[1], groups[2]))
        moved = [pltpu.roll(lines, (8 * (HALF - t)) % 128, 1) if t != HALF else lines for t in range(TAPS)]
        spot24 = lane24 % 8
        for r in range(RANK):
            over_z = None
            for t in range(TAPS):
                term = kz[r][t] * moved[t]
                over_z = term if over_z is None else over_z + term
            total = None
            for d in range(HALF):
                below = pltpu.roll(over_z, 128 - d, 1) if d else over_z
                above = pltpu.roll(over_z, d, 1) if d else over_z
                below = jnp.where(spot24 + d <= 3, below, 0.0)
                above = jnp.where(spot24 - d >= 4, above, 0.0)
                term = kx[r][d] * below + kx[r][TAPS - 1 - d] * above
                total = term if total is None else total + term
            after_z[r, 0, 0:24] = total
            after_z[r, 0, 24:32] = total[0:8]
        beyond = y_lines(ky, 0)
        beyond = jnp.where((lane16 % 8) < 4, pltpu.roll(beyond, 124, 1), pltpu.roll(beyond, 4, 1))
        at_edge = jnp.logical_or(lane16 < 4, lane16 >= 124)
        pack = jnp.zeros((16, 128), F32)
        for z in range(8):
            add = pltpu.roll(beyond, 128 - (8 * (z + 4) + 4), 1)
            plane = use(z, part[z] + jnp.where(at_edge, add, 0.0))
            pack = packed(pack, plane, z)
        return pack

    pack = jnp.zeros((16, 128), F32)
    for z in range(8):
        plane = est_ref[z]
        field[0, 4 + z, 8:24] = plane
        pack = packed(pack, plane, z)
    edge_out[0] = pack

    pl.semaphore_wait(barrier, len(AROUND))

    send_halos(0)
    for copy in raw_copies(0):
        copy.start()

    def view_step(view, carry):
        norm = norm_of(view)

        def to_ratio(z, total):
            plane = data[z] / (total * norm)
            field[1, 4 + z, 8:24] = plane
            return plane

        edge_out[1] = blur(0, view, False, to_ratio, lambda: make_data(view))
        send_halos(1)

        @pl.when(view < views - 1)
        def _():
            for copy in raw_copies(view + 1):
                copy.start()

        def to_current(z, total):
            plane = field[0, 4 + z, 8:24] * (total * norm)
            field[0, 4 + z, 8:24] = plane
            out_ref[z] = plane
            return plane

        edge_out[0] = blur(1, view, True, to_current, lambda: None)

        @pl.when(view < views - 1)
        def _():
            send_halos(0)

        return carry

    lax.fori_loop(0, views, view_step, 0)


def solution(mesh):
    sizes = dict(mesh.shape)

    def shards(raw_views, interp_weight, sample_index, psf, estimate):
        vmem = pl.BlockSpec(memory_space=pltpu.VMEM)
        smem = pl.BlockSpec(memory_space=pltpu.SMEM)
        views = raw_views.shape[0]

        def body(*refs):
            kernel(sizes, *refs)

        return pl.pallas_call(
            body,
            out_shape=jax.ShapeDtypeStruct(estimate.shape, F32),
            in_specs=[smem, vmem, vmem, vmem, vmem],
            out_specs=vmem,
            scratch_shapes=[
                pltpu.VMEM((2, 16, 32, 128), F32),
                pltpu.VMEM((2, 16, 128), F32),
                pltpu.VMEM((2, 2, 3, 3, 16, 128), F32),
                pltpu.VMEM((8, 16, 128), F32),
                pltpu.VMEM((RANK, 16, 24, 128), F32),
                pltpu.VMEM((RANK, 8, 32, 128), F32),
                pltpu.VMEM((2, views, 8, 16, 128), F32),
                pltpu.VMEM((8, 16, 128), F32),
                pltpu.SemaphoreType.DMA((2, 2)),
                pltpu.SemaphoreType.DMA((2, 2)),
                pltpu.SemaphoreType.DMA((2, views)),
                pltpu.SemaphoreType.DMA((2, views)),
            ],
            compiler_params=pltpu.CompilerParams(collective_id=0, has_side_effects=True),
            name="deconvolve",
        )(psf, interp_weight, sample_index, raw_views, estimate)

    return jax.shard_map(
        shards,
        mesh=mesh,
        in_specs=(P(None, "gz", "gy", "gx"), P(), P(), P(), P("gz", "gy", "gx")),
        out_specs=P("gz", "gy", "gx"),
        check_vma=False,
    )
```

```python
import jax
import jax.numpy as jnp
from jax import lax
from jax.experimental import pallas as pl
from jax.experimental.pallas import tpu as pltpu
from jax.sharding import PartitionSpec as P

MESH = pl.DeviceIdType.MESH
F32 = jnp.float32
STEPS = (-1, 0, 1)
AROUND = [(dz, dy, dx) for dx in STEPS for dz in STEPS for dy in STEPS if (dz, dy, dx) != (0, 0, 0)]
AROUND.sort(key=lambda o: (o[2] != 0, -abs(o[0]) - abs(o[1])))
HALF = 4
TAPS = 9
RANK = 4


def window(ref, slot, dz, dy, arriving):
    planes = {
        0: (4, 8),
        1: (12, 4) if arriving else (8, 4),
        -1: (0, 4) if arriving else (4, 4),
    }[dz]
    rows = {
        0: (8, 16),
        1: (24, 4) if arriving else (20, 4),
        -1: (4, 4) if arriving else (8, 4),
    }[dy]
    return ref.at[slot, pl.ds(*planes), pl.ds(*rows), :]


def kernel(
    sizes,
    psf_ref,
    weight_ref,
    index_ref,
    raw_ref,
    est_ref,
    out_ref,
    field,
    edge_out,
    edge_in,
    part,
    after_x,
    after_z,
    beside,
    data,
    send_sem,
    recv_sem,
    raw_send,
    raw_recv,
):
    views = raw_ref.shape[0]
    spots = [lax.axis_index(a) for a in ("gz", "gy", "gx")]
    here = dict(zip(("gz", "gy", "gx"), spots))

    def peer(dz, dy, dx):
        spot = {}
        for axis, by in (("gz", dz), ("gy", dy), ("gx", dx)):
            spot[axis] = lax.rem(here[axis] + (by + sizes[axis]), sizes[axis])
        return spot

    barrier = pltpu.get_barrier_semaphore()
    for offset in AROUND:
        pl.semaphore_signal(barrier, inc=1, device_id=peer(*offset), device_id_type=MESH)

    lane8 = lax.broadcasted_iota(jnp.int32, (8, 128), 1)
    sub8 = lax.broadcasted_iota(jnp.int32, (8, 128), 0)
    lane16 = lax.broadcasted_iota(jnp.int32, (16, 128), 1)
    lane24 = lax.broadcasted_iota(jnp.int32, (24, 128), 1)
    inside = {}
    for axis in ("gz", "gy", "gx"):
        inside[axis] = (
            (here[axis] > 0).astype(jnp.int32),
            (here[axis] < sizes[axis] - 1).astype(jnp.int32),
        )
    from_right8 = (lane8 % 8) >= 4
    rows_ok = jnp.where(sub8 < 4, inside["gy"][1], inside["gy"][0])
    cols_ok = jnp.where(from_right8, inside["gx"][1], inside["gx"][0])

    def packed(pack, plane, num):
        moved = pltpu.roll(plane, 4 + 8 * num, 1)
        return jnp.where(lane16 // 8 == num, moved, pack)

    peers = {offset: peer(*offset) for offset in AROUND}

    def send_halos(slot):
        for dz, dy, dx in AROUND:
            if dx == 0:
                src = window(field, slot, dz, dy, False)
                dst = window(field, slot, -dz, -dy, True)
            else:
                rows = pl.ds(*{0: (0, 16), 1: (12, 4), -1: (0, 4)}[dy])
                src = edge_out.at[slot, rows]
                dst = edge_in.at[slot, (1 - dx) // 2, 1 - dz, 1 - dy, rows]
            kind = 0 if dx == 0 else 1
            pltpu.make_async_remote_copy(
                src_ref=src,
                dst_ref=dst,
                send_sem=send_sem.at[slot, kind],
                recv_sem=recv_sem.at[slot, kind],
                device_id=peers[dz, dy, dx],
                device_id_type=MESH,
            ).start()

    def wait_halos(slot, kind, sem):
        whole = field.at[slot, :, pl.ds(0, 16), :] if kind == 0 else edge_in.at[slot, 0]
        pltpu.make_async_copy(whole, whole, sem.at[slot, kind]).wait()

    def raw_copies(view):
        return [
            pltpu.make_async_remote_copy(
                src_ref=raw_ref.at[view],
                dst_ref=beside.at[side, view],
                send_sem=raw_send.at[side, view],
                recv_sem=raw_recv.at[side, view],
                device_id=peer(0, 0, by),
                device_id_type=MESH,
            )
            for side, by in ((0, 1), (1, -1))
        ]

    def make_data(view):
        for copy in raw_copies(view):
            copy.wait()
        own = pl.ds(pl.multiple_of(here["gx"] * 128, 128), 128)
        row = lax.broadcasted_iota(jnp.int32, (views, 128), 0)
        first = jnp.sum(jnp.where(row == view, index_ref[:, own], 0), axis=0, keepdims=True)
        weight = jnp.sum(jnp.where(row == view, weight_ref[:, own], 0.0), axis=0, keepdims=True)
        source = lax.broadcasted_iota(jnp.int32, (128, 128), 0)
        total = None
        for brick, ref in ((-1, beside.at[0]), (0, raw_ref), (1, beside.at[1])):
            at = source + (here["gx"] + brick) * 128
            table = jnp.where(at == first, 1.0 - weight, 0.0)
            table = table + jnp.where(at == first + 1, weight, 0.0)
            part = jnp.dot(
                ref[view].reshape(128, 128),
                table,
                precision=lax.Precision.HIGHEST,
                preferred_element_type=F32,
            )
            total = part if total is None else total + part
        data[...] = total.reshape(8, 16, 128)

    def taps(view, axis, flipped):
        return [
            [psf_ref[view, axis, r, TAPS - 1 - t if flipped else t] for t in range(TAPS)]
            for r in range(RANK)
        ]

    def norm_of(view):
        total = 0.0
        for r in range(RANK):
            prod = None
            for axis in range(3):
                line = psf_ref[view, axis, r, 0]
                for t in range(1, TAPS):
                    line = line + psf_ref[view, axis, r, t]
                prod = line if prod is None else prod * line
            total = total + prod
        return 1.0 / jnp.full((16, 128), total, F32)

    def x_lines(lines, kx, store):
        lane = lax.broadcasted_iota(jnp.int32, lines.shape, 1)
        sums = [None] * RANK
        for t in range(TAPS):
            s = t - HALF
            if s == 0:
                moved = lines
            elif s > 0:
                moved = pltpu.roll(jnp.where(lane < s, 0.0, lines), 128 - s, 1)
            else:
                moved = pltpu.roll(jnp.where(lane >= 128 + s, 0.0, lines), -s, 1)
            for r in range(RANK):
                term = kx[r][t] * moved
                sums[r] = term if sums[r] is None else sums[r] + term
        for r in range(RANK):
            store(r, sums[r])

    def y_lines(ky, z):
        total = None
        for r in range(RANK):
            for t in range(TAPS):
                term = ky[r][t] * after_z[r, z, HALF + t : HALF + t + 16]
                total = term if total is None else total + term
        return total

    def edge_rows(slot, z, ok):
        edge = jnp.where(sub8 < 4, field[slot, z, 24:32], field[slot, z, 0:8])
        return jnp.where(jnp.logical_and(rows_ok > 0, ok > 0), edge, 0.0)

    def blur(slot, view, flipped, use, meanwhile):
        kz, ky, kx = [taps(view, axis, flipped) for axis in range(3)]

        def own_step(i, carry):
            for j in range(4):
                z = 4 + i * 4 + j

                def store(r, value):
                    after_x[r, z, 8:24] = value

                x_lines(field[slot, z, 8:24], kx, store)
            return carry

        lax.fori_loop(0, 2, own_step, 0)
        meanwhile()
        wait_halos(slot, 0, recv_sem)

        def far_step(i, carry):
            ok = jnp.where(i == 0, inside["gz"][0], inside["gz"][1])
            ok8 = jnp.full((8, 128), ok, jnp.int32)
            ok16 = jnp.full((16, 128), ok, jnp.int32)
            for j in range(4):
                z = 12 * i + j
                own = jnp.where(ok16 > 0, field[slot, z, 8:24], 0.0)
                lines = jnp.concatenate([edge_rows(slot, z, ok8), own], axis=0)

                def store(r, value):
                    after_x[r, z] = value

                x_lines(lines, kx, store)
            return carry

        lax.fori_loop(0, 2, far_step, 0, unroll=True)
        always = jnp.full((8, 128), 1, jnp.int32)

        def near_step(i, carry):
            for j in range(4):
                z = 4 + i * 4 + j

                def store(r, value):
                    after_x[r, z, 0:8] = value

                x_lines(edge_rows(slot, z, always), kx, store)
            return carry

        lax.fori_loop(0, 2, near_step, 0, unroll=True)

        def z_step(z, carry):
            for r in range(RANK):
                total = kz[r][0] * after_x[r, z]
                for t in range(1, TAPS):
                    total = total + kz[r][t] * after_x[r, z + t]
                after_z[r, z, 0:24] = total
                after_z[r, z, 24:32] = total[0:8]
            return carry

        lax.fori_loop(0, 8, z_step, 0, unroll=2)

        def y_step(z, carry):
            part[z] = y_lines(ky, z)
            return carry

        lax.fori_loop(0, 8, y_step, 0, unroll=4)
        wait_halos(slot, 1, recv_sem)
        wait_halos(slot, 0, send_sem)
        wait_halos(slot, 1, send_sem)

        groups = []
        for dz in range(3):
            seen = []
            for dy in range(3):
                left, right = edge_in[slot, 0, dz, dy], edge_in[slot, 1, dz, dy]
                seen.append(jnp.where((lane16 % 8) >= 4, right, left))
            ok = (inside["gz"][0], 1, inside["gz"][1])[dz]
            ok8 = jnp.logical_and(jnp.full((8, 128), ok, jnp.int32) > 0, cols_ok > 0)
            edge = jnp.where(sub8 < 4, seen[2][0:8], seen[0][8:16])
            edge = jnp.where(jnp.logical_and(rows_ok > 0, ok8), edge, 0.0)
            rows = [edge] + [jnp.where(ok8, seen[1][8 * h : 8 * h + 8], 0.0) for h in range(2)]
            groups.append(pltpu.roll(jnp.concatenate(rows, axis=0), (96, 32, 96)[dz], 1))
        lines = jnp.where(lane24 < 32, groups[0], jnp.where(lane24 < 96, groups[1], groups[2]))
        moved = [pltpu.roll(lines, (8 * (HALF - t)) % 128, 1) if t != HALF else lines for t in range(TAPS)]
        spot24 = lane24 % 8
        for r in range(RANK):
            over_z = None
            for t in range(TAPS):
                term = kz[r][t] * moved[t]
                over_z = term if over_z is None else over_z + term
            total = None
            for d in range(HALF):
                below = pltpu.roll(over_z, 128 - d, 1) if d else over_z
                above = pltpu.roll(over_z, d, 1) if d else over_z
                below = jnp.where(spot24 + d <= 3, below, 0.0)
                above = jnp.where(spot24 - d >= 4, above, 0.0)
                term = kx[r][d] * below + kx[r][TAPS - 1 - d] * above
                total = term if total is None else total + term
            after_z[r, 0, 0:24] = total
            after_z[r, 0, 24:32] = total[0:8]
        beyond = y_lines(ky, 0)
        beyond = jnp.where((lane16 % 8) < 4, pltpu.roll(beyond, 124, 1), pltpu.roll(beyond, 4, 1))
        at_edge = jnp.logical_or(lane16 < 4, lane16 >= 124)
        pack = jnp.zeros((16, 128), F32)
        for z in range(8):
            add = pltpu.roll(beyond, 128 - (8 * (z + 4) + 4), 1)
            plane = use(z, part[z] + jnp.where(at_edge, add, 0.0))
            pack = packed(pack, plane, z)
        return pack

    pack = jnp.zeros((16, 128), F32)
    for z in range(8):
        plane = est_ref[z]
        field[0, 4 + z, 8:24] = plane
        pack = packed(pack, plane, z)
    edge_out[0] = pack

    pl.semaphore_wait(barrier, len(AROUND))

    send_halos(0)
    for copy in raw_copies(0):
        copy.start()

    def view_step(view, carry):
        norm = norm_of(view)

        def to_ratio(z, total):
            plane = data[z] / (total * norm)
            field[1, 4 + z, 8:24] = plane
            return plane

        edge_out[1] = blur(0, view, False, to_ratio, lambda: make_data(view))
        send_halos(1)

        @pl.when(view < views - 1)
        def _():
            for copy in raw_copies(view + 1):
                copy.start()

        def to_current(z, total):
            plane = field[0, 4 + z, 8:24] * (total * norm)
            field[0, 4 + z, 8:24] = plane
            out_ref[z] = plane
            return plane

        edge_out[0] = blur(1, view, True, to_current, lambda: None)

        @pl.when(view < views - 1)
        def _():
            send_halos(0)

        return carry

    lax.fori_loop(0, views, view_step, 0)


def solution(mesh):
    sizes = dict(mesh.shape)

    def shards(raw_views, interp_weight, sample_index, psf, estimate):
        vmem = pl.BlockSpec(memory_space=pltpu.VMEM)
        smem = pl.BlockSpec(memory_space=pltpu.SMEM)
        views = raw_views.shape[0]

        def body(*refs):
            kernel(sizes, *refs)

        return pl.pallas_call(
            body,
            out_shape=jax.ShapeDtypeStruct(estimate.shape, F32),
            in_specs=[smem, vmem, vmem, vmem, vmem],
            out_specs=vmem,
            scratch_shapes=[
                pltpu.VMEM((2, 16, 32, 128), F32),
                pltpu.VMEM((2, 16, 128), F32),
                pltpu.VMEM((2, 2, 3, 3, 16, 128), F32),
                pltpu.VMEM((8, 16, 128), F32),
                pltpu.VMEM((RANK, 16, 24, 128), F32),
                pltpu.VMEM((RANK, 8, 32, 128), F32),
                pltpu.VMEM((2, views, 8, 16, 128), F32),
                pltpu.VMEM((8, 16, 128), F32),
                pltpu.SemaphoreType.DMA((2, 2)),
                pltpu.SemaphoreType.DMA((2, 2)),
                pltpu.SemaphoreType.DMA((2, views)),
                pltpu.SemaphoreType.DMA((2, views)),
            ],
            compiler_params=pltpu.CompilerParams(collective_id=0, has_side_effects=True),
            name="deconvolve",
        )(psf, interp_weight, sample_index, raw_views, estimate)

    return jax.shard_map(
        shards,
        mesh=mesh,
        in_specs=(P(None, "gz", "gy", "gx"), P(), P(), P(), P("gz", "gy", "gx")),
        out_specs=P("gz", "gy", "gx"),
        check_vma=False,
    )
```

```python
import jax
import jax.numpy as jnp
from jax import lax
from jax.experimental import pallas as pl
from jax.experimental.pallas import tpu as pltpu
from jax.sharding import PartitionSpec as P

MESH = pl.DeviceIdType.MESH
F32 = jnp.float32
STEPS = (-1, 0, 1)
AROUND = [(dz, dy, dx) for dx in STEPS for dz in STEPS for dy in STEPS if (dz, dy, dx) != (0, 0, 0)]
AROUND.sort(key=lambda o: (o[2] != 0, -abs(o[0]) - abs(o[1])))
HALF = 4
TAPS = 9
RANK = 4


def window(ref, slot, dz, dy, arriving):
    planes = {
        0: (4, 8),
        1: (12, 4) if arriving else (8, 4),
        -1: (0, 4) if arriving else (4, 4),
    }[dz]
    rows = {
        0: (8, 16),
        1: (24, 4) if arriving else (20, 4),
        -1: (4, 4) if arriving else (8, 4),
    }[dy]
    return ref.at[slot, pl.ds(*planes), pl.ds(*rows), :]


def kernel(
    sizes,
    psf_ref,
    weight_ref,
    index_ref,
    raw_ref,
    est_ref,
    out_ref,
    field,
    edge_out,
    edge_in,
    part,
    after_x,
    after_z,
    beside,
    data,
    send_sem,
    recv_sem,
    raw_send,
    raw_recv,
):
    views = raw_ref.shape[0]
    spots = [lax.axis_index(a) for a in ("gz", "gy", "gx")]
    here = dict(zip(("gz", "gy", "gx"), spots))

    def peer(dz, dy, dx):
        spot = {}
        for axis, by in (("gz", dz), ("gy", dy), ("gx", dx)):
            spot[axis] = lax.rem(here[axis] + (by + sizes[axis]), sizes[axis])
        return spot

    barrier = pltpu.get_barrier_semaphore()
    for offset in AROUND:
        pl.semaphore_signal(barrier, inc=1, device_id=peer(*offset), device_id_type=MESH)

    lane8 = lax.broadcasted_iota(jnp.int32, (8, 128), 1)
    sub8 = lax.broadcasted_iota(jnp.int32, (8, 128), 0)
    lane16 = lax.broadcasted_iota(jnp.int32, (16, 128), 1)
    lane24 = lax.broadcasted_iota(jnp.int32, (24, 128), 1)
    inside = {}
    for axis in ("gz", "gy", "gx"):
        inside[axis] = (
            (here[axis] > 0).astype(jnp.int32),
            (here[axis] < sizes[axis] - 1).astype(jnp.int32),
        )
    from_right8 = (lane8 % 8) >= 4
    rows_ok = jnp.where(sub8 < 4, inside["gy"][1], inside["gy"][0])
    cols_ok = jnp.where(from_right8, inside["gx"][1], inside["gx"][0])

    def packed(pack, plane, num):
        moved = pltpu.roll(plane, 4 + 8 * num, 1)
        return jnp.where(lane16 // 8 == num, moved, pack)

    peers = {offset: peer(*offset) for offset in AROUND}

    def send_halos(slot):
        for dz, dy, dx in AROUND:
            if dx == 0:
                src = window(field, slot, dz, dy, False)
                dst = window(field, slot, -dz, -dy, True)
            else:
                rows = pl.ds(*{0: (0, 16), 1: (12, 4), -1: (0, 4)}[dy])
                src = edge_out.at[slot, rows]
                dst = edge_in.at[slot, (1 - dx) // 2, 1 - dz, 1 - dy, rows]
            kind = 0 if dx == 0 else 1
            pltpu.make_async_remote_copy(
                src_ref=src,
                dst_ref=dst,
                send_sem=send_sem.at[slot, kind],
                recv_sem=recv_sem.at[slot, kind],
                device_id=peers[dz, dy, dx],
                device_id_type=MESH,
            ).start()

    def wait_halos(slot, kind, sem):
        whole = field.at[slot, :, pl.ds(0, 16), :] if kind == 0 else edge_in.at[slot, 0]
        pltpu.make_async_copy(whole, whole, sem.at[slot, kind]).wait()

    def raw_copies(view):
        return [
            pltpu.make_async_remote_copy(
                src_ref=raw_ref.at[view],
                dst_ref=beside.at[side, view],
                send_sem=raw_send.at[side, view],
                recv_sem=raw_recv.at[side, view],
                device_id=peer(0, 0, by),
                device_id_type=MESH,
            )
            for side, by in ((0, 1), (1, -1))
        ]

    def make_data(view):
        for copy in raw_copies(view):
            copy.wait()
        own = pl.ds(pl.multiple_of(here["gx"] * 128, 128), 128)
        row = lax.broadcasted_iota(jnp.int32, (views, 128), 0)
        first = jnp.sum(jnp.where(row == view, index_ref[:, own], 0), axis=0, keepdims=True)
        weight = jnp.sum(jnp.where(row == view, weight_ref[:, own], 0.0), axis=0, keepdims=True)
        source = lax.broadcasted_iota(jnp.int32, (128, 128), 0)
        total = None
        for brick, ref in ((-1, beside.at[0]), (0, raw_ref), (1, beside.at[1])):
            at = source + (here["gx"] + brick) * 128
            table = jnp.where(at == first, 1.0 - weight, 0.0)
            table = table + jnp.where(at == first + 1, weight, 0.0)
            part = jnp.dot(
                ref[view].reshape(128, 128),
                table,
                precision=lax.Precision.HIGHEST,
                preferred_element_type=F32,
            )
            total = part if total is None else total + part
        data[...] = total.reshape(8, 16, 128)

    def taps(view, axis, flipped):
        return [
            [psf_ref[view, axis, r, TAPS - 1 - t if flipped else t] for t in range(TAPS)]
            for r in range(RANK)
        ]

    def norm_of(view):
        total = 0.0
        for r in range(RANK):
            prod = None
            for axis in range(3):
                line = psf_ref[view, axis, r, 0]
                for t in range(1, TAPS):
                    line = line + psf_ref[view, axis, r, t]
                prod = line if prod is None else prod * line
            total = total + prod
        return 1.0 / jnp.full((16, 128), total, F32)

    def x_lines(lines, kx, store):
        lane = lax.broadcasted_iota(jnp.int32, lines.shape, 1)
        sums = [None] * RANK
        for t in range(TAPS):
            s = t - HALF
            if s == 0:
                moved = lines
            elif s > 0:
                moved = pltpu.roll(jnp.where(lane < s, 0.0, lines), 128 - s, 1)
            else:
                moved = pltpu.roll(jnp.where(lane >= 128 + s, 0.0, lines), -s, 1)
            for r in range(RANK):
                term = kx[r][t] * moved
                sums[r] = term if sums[r] is None else sums[r] + term
        for r in range(RANK):
            store(r, sums[r])

    def y_lines(ky, z):
        total = None
        for r in range(RANK):
            for t in range(TAPS):
                term = ky[r][t] * after_z[r, z, HALF + t : HALF + t + 16]
                total = term if total is None else total + term
        return total

    def edge_rows(slot, z, ok):
        edge = jnp.where(sub8 < 4, field[slot, z, 24:32], field[slot, z, 0:8])
        return jnp.where(jnp.logical_and(rows_ok > 0, ok > 0), edge, 0.0)

    def blur(slot, view, flipped, use, meanwhile):
        kz, ky, kx = [taps(view, axis, flipped) for axis in range(3)]

        def own_step(i, carry):
            for j in range(4):
                z = 4 + i * 4 + j

                def store(r, value):
                    after_x[r, z, 8:24] = value

                x_lines(field[slot, z, 8:24], kx, store)
            return carry

        lax.fori_loop(0, 2, own_step, 0)
        meanwhile()
        wait_halos(slot, 0, recv_sem)

        def far_step(i, carry):
            ok = jnp.where(i == 0, inside["gz"][0], inside["gz"][1])
            ok8 = jnp.full((8, 128), ok, jnp.int32)
            ok16 = jnp.full((16, 128), ok, jnp.int32)
            for j in range(4):
                z = 12 * i + j
                own = jnp.where(ok16 > 0, field[slot, z, 8:24], 0.0)
                lines = jnp.concatenate([edge_rows(slot, z, ok8), own], axis=0)

                def store(r, value):
                    after_x[r, z] = value

                x_lines(lines, kx, store)
            return carry

        lax.fori_loop(0, 2, far_step, 0, unroll=True)
        always = jnp.full((8, 128), 1, jnp.int32)

        def near_step(i, carry):
            for j in range(4):
                z = 4 + i * 4 + j

                def store(r, value):
                    after_x[r, z, 0:8] = value

                x_lines(edge_rows(slot, z, always), kx, store)
            return carry

        lax.fori_loop(0, 2, near_step, 0, unroll=True)

        def z_step(z, carry):
            for r in range(RANK):
                total = kz[r][0] * after_x[r, z]
                for t in range(1, TAPS):
                    total = total + kz[r][t] * after_x[r, z + t]
                after_z[r, z, 0:24] = total
                after_z[r, z, 24:32] = total[0:8]
            return carry

        lax.fori_loop(0, 8, z_step, 0, unroll=2)

        def y_step(z, carry):
            part[z] = y_lines(ky, z)
            return carry

        lax.fori_loop(0, 8, y_step, 0, unroll=4)
        wait_halos(slot, 1, recv_sem)
        wait_halos(slot, 0, send_sem)
        wait_halos(slot, 1, send_sem)

        groups = []
        for dz in range(3):
            seen = []
            for dy in range(3):
                left, right = edge_in[slot, 0, dz, dy], edge_in[slot, 1, dz, dy]
                seen.append(jnp.where((lane16 % 8) >= 4, right, left))
            ok = (inside["gz"][0], 1, inside["gz"][1])[dz]
            ok8 = jnp.logical_and(jnp.full((8, 128), ok, jnp.int32) > 0, cols_ok > 0)
            edge = jnp.where(sub8 < 4, seen[2][0:8], seen[0][8:16])
            edge = jnp.where(jnp.logical_and(rows_ok > 0, ok8), edge, 0.0)
            rows = [edge] + [jnp.where(ok8, seen[1][8 * h : 8 * h + 8], 0.0) for h in range(2)]
            groups.append(pltpu.roll(jnp.concatenate(rows, axis=0), (96, 32, 96)[dz], 1))
        lines = jnp.where(lane24 < 32, groups[0], jnp.where(lane24 < 96, groups[1], groups[2]))
        moved = [pltpu.roll(lines, (8 * (HALF - t)) % 128, 1) if t != HALF else lines for t in range(TAPS)]
        spot24 = lane24 % 8
        for r in range(RANK):
            over_z = None
            for t in range(TAPS):
                term = kz[r][t] * moved[t]
                over_z = term if over_z is None else over_z + term
            total = None
            for d in range(HALF):
                below = pltpu.roll(over_z, 128 - d, 1) if d else over_z
                above = pltpu.roll(over_z, d, 1) if d else over_z
                below = jnp.where(spot24 + d <= 3, below, 0.0)
                above = jnp.where(spot24 - d >= 4, above, 0.0)
                term = kx[r][d] * below + kx[r][TAPS - 1 - d] * above
                total = term if total is None else total + term
            after_z[r, 0, 0:24] = total
            after_z[r, 0, 24:32] = total[0:8]
        beyond = y_lines(ky, 0)
        beyond = jnp.where((lane16 % 8) < 4, pltpu.roll(beyond, 124, 1), pltpu.roll(beyond, 4, 1))
        at_edge = jnp.logical_or(lane16 < 4, lane16 >= 124)
        pack = jnp.zeros((16, 128), F32)
        for z in range(8):
            add = pltpu.roll(beyond, 128 - (8 * (z + 4) + 4), 1)
            plane = use(z, part[z] + jnp.where(at_edge, add, 0.0))
            pack = packed(pack, plane, z)
        return pack

    pack = jnp.zeros((16, 128), F32)
    for z in range(8):
        plane = est_ref[z]
        field[0, 4 + z, 8:24] = plane
        pack = packed(pack, plane, z)
    edge_out[0] = pack

    first_norm = norm_of(0)
    pl.semaphore_wait(barrier, len(AROUND))

    send_halos(0)
    for copy in raw_copies(0):
        copy.start()

    def view_step(view, norm):
        following = []

        def to_ratio(z, total):
            plane = data[z] / (total * norm)
            field[1, 4 + z, 8:24] = plane
            return plane

        edge_out[1] = blur(0, view, False, to_ratio, lambda: make_data(view))
        send_halos(1)

        @pl.when(view < views - 1)
        def _():
            for copy in raw_copies(view + 1):
                copy.start()

        def to_current(z, total):
            plane = field[0, 4 + z, 8:24] * (total * norm)
            field[0, 4 + z, 8:24] = plane
            out_ref[z] = plane
            return plane

        edge_out[0] = blur(1, view, True, to_current, lambda: following.append(norm_of(lax.min(view + 1, views - 1))))

        @pl.when(view < views - 1)
        def _():
            send_halos(0)

        return following[0]

    lax.fori_loop(0, views, view_step, first_norm)


def solution(mesh):
    sizes = dict(mesh.shape)

    def shards(raw_views, interp_weight, sample_index, psf, estimate):
        vmem = pl.BlockSpec(memory_space=pltpu.VMEM)
        smem = pl.BlockSpec(memory_space=pltpu.SMEM)
        views = raw_views.shape[0]

        def body(*refs):
            kernel(sizes, *refs)

        return pl.pallas_call(
            body,
            out_shape=jax.ShapeDtypeStruct(estimate.shape, F32),
            in_specs=[smem, vmem, vmem, vmem, vmem],
            out_specs=vmem,
            scratch_shapes=[
                pltpu.VMEM((2, 16, 32, 128), F32),
                pltpu.VMEM((2, 16, 128), F32),
                pltpu.VMEM((2, 2, 3, 3, 16, 128), F32),
                pltpu.VMEM((8, 16, 128), F32),
                pltpu.VMEM((RANK, 16, 24, 128), F32),
                pltpu.VMEM((RANK, 8, 32, 128), F32),
                pltpu.VMEM((2, views, 8, 16, 128), F32),
                pltpu.VMEM((8, 16, 128), F32),
                pltpu.SemaphoreType.DMA((2, 2)),
                pltpu.SemaphoreType.DMA((2, 2)),
                pltpu.SemaphoreType.DMA((2, views)),
                pltpu.SemaphoreType.DMA((2, views)),
            ],
            compiler_params=pltpu.CompilerParams(collective_id=0, has_side_effects=True),
            name="deconvolve",
        )(psf, interp_weight, sample_index, raw_views, estimate)

    return jax.shard_map(
        shards,
        mesh=mesh,
        in_specs=(P(None, "gz", "gy", "gx"), P(), P(), P(), P("gz", "gy", "gx")),
        out_specs=P("gz", "gy", "gx"),
        check_vma=False,
    )
```
